256 devices in a mesh: seq: 32 (over x, y, core), head: 8 (over z).
Axes of the slice: x: 4, y: 4, z: 8, core: 2. Of those that a mesh axis runs over, the one named last changes fastest.
Arguments:
- query_rows: bfloat16 [4096, 3072], P('seq', 'head'), may hold values from -30 to 30
- key_rows: bfloat16 [4096, 3072], P('seq', 'head'), may hold values from -22.5 to 22.5
- value_rows: bfloat16 [4096, 3072], P('seq', 'head'), may hold values from -6 to 6
- output_grad: bfloat16 [4096, 5120], P('seq', 'head'), may hold values from -6 to 6
- out_weight: bfloat16 [5120, 3072], P(None, 'head'), may hold values from -0.078125 to 0.078125
- clusters: int32 [64], replicated, may hold values from 0 to 3
Outputs:
- query_grad: bfloat16 [4096, 3072], P('seq', 'head')
- key_grad: bfloat16 [4096, 3072], P('seq', 'head')
- value_grad: bfloat16 [4096, 3072], P('seq', 'head')
The draws below stay inside these ranges and needn't reach their ends.
Inputs may be any that keep to these rules, and one draw needn't show every extreme that they name: `clusters`: cluster of each block of 64 tokens.
All inputs are finite; a program needn't handle non-finite values.
Results may differ from the reference program's by a relative error of at most 0.023.
Values may be sent and summed in bfloat16 or wider, within the bound.
No kernel may reach another device: no remote copies, remote signals or barrier semaphores. Data moves between devices by JAX's collectives and lax.ppermute only.
A program may use at most 64 MiB of HBM per device.

```python
import jax
import jax.numpy as jnp
from jax import lax

D = 5120
HEADS = 24
HS = 128
BLK = 64
CLUSTERS = 4
TOKENS = 4096
NBLK = 64


def paired_keys(key):
    base = jnp.clip(jax.random.normal(jax.random.fold_in(key, 11), (TOKENS, HEADS * HS), jnp.float32), -4.5, 4.5)
    return base


def draw_key_rows(key, part):
    return paired_keys(key).astype(jnp.bfloat16)


def draw_query_rows(key, part):
    base = jnp.clip(jax.random.normal(jax.random.fold_in(key, 12), (TOKENS, HEADS * HS), jnp.float32), -4.5, 4.5)
    return base.astype(jnp.bfloat16)


def set_ends(values, own_key, smallest, top_value):
    dims = values.shape
    spot = [jax.random.randint(jax.random.fold_in(own_key, axis), (), 0, dims[axis]) for axis in range(len(dims))]
    values = values.at[tuple(spot)].set(smallest)
    longest = dims.index(max(dims))
    spot[longest] = (spot[longest] + 1) % dims[longest]
    return values.at[tuple(spot)].set(top_value)


def levels(rng, dims, cuts, least, high):
    loudness, own = 1.0, jax.random.fold_in(rng, 6)
    for dim, blocks in cuts:
        heights = jnp.exp(jax.random.uniform(jax.random.fold_in(own, dim), (blocks,), jnp.float32, least / len(cuts), high / len(cuts)))
        loudness = loudness * jnp.repeat(heights, dims[dim] // blocks).reshape([-1 if axis == dim else 1 for axis in range(len(dims))])
    return loudness


def gaussian(own_key, shape, deviation, most, cuts=(), kind=jnp.bfloat16):
    array = deviation * jax.random.normal(own_key, shape, jnp.float32)
    if cuts:
        array = array * levels(own_key, shape, cuts, -0.22, 0.18)
    return jnp.clip(array, -most, most).astype(kind)


def setup_inputs(seed: int = 0) -> dict:
    key_list = jax.random.split(jax.random.key(seed), 7)
    return {
        "query_rows": draw_query_rows(jax.random.fold_in(key_list[6], 71), 0),
        "key_rows": draw_key_rows(jax.random.fold_in(key_list[6], 71), 0),
        "value_rows": gaussian(key_list[2], (TOKENS, HEADS * HS), 1.0, 6.0, ((0, 32), (1, 8))),
        "output_grad": gaussian(key_list[3], (TOKENS, D), 1.0, 6.0, ((0, 32), (1, 8))),
        "out_weight": gaussian(key_list[4], (D, HEADS * HS), D ** -0.5, 0.078125, ((1, 8),)),
        "clusters": set_ends(jax.random.randint(key_list[5], (NBLK,), 0, CLUSTERS), jax.random.fold_in(key_list[5], 1), 0, CLUSTERS - 1).astype(jnp.int32),
    }


def split_heads(matrix):
    return matrix.reshape(TOKENS, HEADS, HS).transpose(1, 0, 2)


def join_heads(stacked):
    return stacked.transpose(1, 0, 2).reshape(TOKENS, HEADS * HS)


def reference(query_rows, key_rows, value_rows, output_grad, out_weight, clusters):
    score_scale = HS ** -0.5
    positions = jnp.arange(TOKENS, dtype=jnp.int32)
    token_cluster = clusters[positions // BLK]
    allowed = (token_cluster[:, None] == token_cluster[None, :]) & (positions[None, :] <= positions[:, None])

    def head_scores(query_head, key_head):
        scores = jnp.dot(query_head, key_head.T, preferred_element_type=jnp.float32) * score_scale
        return jnp.where(allowed, scores, -jnp.inf)

    def forward(triple):
        query_head, key_head, value_head = triple
        scores = head_scores(query_head, key_head)
        row_max = jnp.max(scores, axis=1, keepdims=True)
        row_total = jnp.sum(jnp.exp(scores - row_max), axis=1, keepdims=True)
        log_total = row_max + jnp.log(row_total)
        probability_b = jnp.exp(scores - log_total).astype(jnp.bfloat16)
        attended = jnp.dot(probability_b, value_head, preferred_element_type=jnp.float32).astype(jnp.bfloat16)
        return attended, log_total[:, 0]

    query_heads = split_heads(query_rows)
    key_heads = split_heads(key_rows)
    value_heads = split_heads(value_rows)
    attended, log_totals = lax.map(forward, (query_heads, key_heads, value_heads))
    grad_attended = jnp.dot(output_grad, out_weight, preferred_element_type=jnp.float32).astype(jnp.bfloat16)
    grad_heads = split_heads(grad_attended)

    def backward(items):
        query_head, key_head, value_head, attended_head, grad_head, log_head = items
        scores = head_scores(query_head, key_head)
        probability = jnp.exp(scores - log_head[:, None])
        correction = jnp.sum(grad_head.astype(jnp.float32) * attended_head.astype(jnp.float32), axis=1, keepdims=True)
        grad_prob = jnp.dot(grad_head, value_head.T, preferred_element_type=jnp.float32)
        grad_score = (probability * (grad_prob - correction) * score_scale).astype(jnp.bfloat16)
        query_grad = jnp.dot(grad_score, key_head, preferred_element_type=jnp.float32).astype(jnp.bfloat16)
        key_grad = jnp.dot(grad_score.T, query_head, preferred_element_type=jnp.float32).astype(jnp.bfloat16)
        value_grad = jnp.dot(probability.astype(jnp.bfloat16).T, grad_head, preferred_element_type=jnp.float32).astype(jnp.bfloat16)
        return query_grad, key_grad, value_grad

    query_grad, key_grad, value_grad = lax.map(backward, (query_heads, key_heads, value_heads, attended, grad_heads, log_totals))
    return join_heads(query_grad), join_heads(key_grad), join_heads(value_grad)
```

```python
import functools

import jax
import jax.numpy as jnp
from jax import lax
from jax.experimental import pallas as pl
from jax.experimental.pallas import tpu as pltpu
from jax.sharding import PartitionSpec as P

HS = 128
BLK = 64
XS, YS, CS = 4, 4, 2
NSEQ = XS * YS * CS
NZ = 8
HEADS_HERE = 3
ROWS = 128
NBLK = 64
TOK = NBLK * BLK
WIN = 8
PAD = TOK + WIN * BLK
TILE = 256
SCALE = HS**-0.5
SCALE2 = SCALE * 1.4426950408889634
NEG = -1e30


f32, bf16 = jnp.float32, jnp.bfloat16
VM = pl.BlockSpec(memory_space=pltpu.VMEM)
SM = pl.BlockSpec(memory_space=pltpu.SMEM)


def seq_id(x, y, c):
    return ((x % XS) * YS + (y % YS)) * CS + (c % CS)


COORDS = [(x, y, c) for x in range(XS) for y in range(YS) for c in range(CS)]


def to_heads(a, d):
    pairs = [
        (seq_id(x, y, c), seq_id(x, y + d, c))
        for x, y, c in COORDS
        if (y + d) % YS < HEADS_HERE
    ]
    return lax.ppermute(a, "seq", pairs)


def from_heads(a, d):
    pairs = [
        (seq_id(x, y, c), seq_id(x, y - d, c)) for x, y, c in COORDS if y < HEADS_HERE
    ]
    return lax.ppermute(a, "seq", pairs)


def along_x(a, d):
    pairs = [
        (seq_id(x, y, c), seq_id(x + d, y, c)) for x, y, c in COORDS if y < HEADS_HERE
    ]
    return lax.ppermute(a, "seq", pairs)


def swap_core(a):
    pairs = [
        (seq_id(x, y, c), seq_id(x, y, c + 1)) for x, y, c in COORDS if y < HEADS_HERE
    ]
    return lax.ppermute(a, "seq", pairs)


def along_z(a, d):
    return lax.ppermute(a, "head", [(z, (z + d) % NZ) for z in range(NZ)])


def nt(a, b):
    return lax.dot_general(a, b, (((1,), (1,)), ((), ())), preferred_element_type=f32)


def nn(a, b):
    return lax.dot_general(a, b, (((1,), (0,)), ((), ())), preferred_element_type=f32)


def head_slice(y, d):
    head = jnp.minimum(lax.rem(y + d, YS), HEADS_HERE - 1)
    return pl.ds(pl.multiple_of(head * HS, HS), HS)


def pack_kernel(pos, q, k, v, *outs):
    y = pos[0]
    for d in range(YS):
        cols = head_slice(y, d)
        outs[d][:, 0:HS] = q[:, cols]
        outs[d][:, HS : 2 * HS] = k[:, cols]
        outs[d][:, 2 * HS :] = v[:, cols]


def project_kernel(pos, *refs):
    parts, w, outs, keep = refs[:8], refs[8], refs[9:13], refs[13]
    y, z = pos[0], pos[1]
    depth = parts[0].shape[1]
    total = None
    for d in range(NZ):
        start = pl.multiple_of(lax.rem(z - d + NZ, NZ) * depth, depth)
        term = nn(parts[d][...], w[pl.ds(start, depth), :])
        total = term if total is None else total + term
    keep[...] = total.astype(bf16)
    for d in range(YS):
        outs[d][...] = keep[:, head_slice(y, d)]


def forward_kernel(tab, *refs):
    arrays = refs[:8]
    qs, ks, vs, att, lse_c, lse_r = refs[8:]
    active = tab[3, 0]
    for a in range(8):

        def place(i, _, a=a):
            src = pl.ds(pl.multiple_of(i * BLK, BLK), BLK)
            dst = pl.ds(pl.multiple_of(tab[0, a * 8 + i] * BLK, BLK), BLK)
            qs[dst, :] = arrays[a][src, 0:HS]
            ks[dst, :] = arrays[a][src, HS : 2 * HS]
            vs[dst, :] = arrays[a][src, 2 * HS :]
            return 0

        lax.fori_loop(0, 8, place, 0, unroll=True)
    tail = pl.ds(TOK, PAD - TOK)
    for ref in (qs, ks, vs):
        ref[tail, :] = jnp.zeros((PAD - TOK, HS), bf16)
    lse_r[:, tail] = jnp.zeros((8, PAD - TOK), f32)
    row = lax.broadcasted_iota(jnp.int32, (TILE, TILE), 0)
    col = lax.broadcasted_iota(jnp.int32, (TILE, TILE), 1)
    per = TILE // BLK

    def q_tile(t, _):
        base = pl.multiple_of(t * TILE, TILE)
        qt = qs[pl.ds(base, TILE), :]
        low = jnp.full((TILE, TILE), tab[1, t * per] * BLK, jnp.int32)
        for i in range(1, per):
            low = jnp.where(row >= i * BLK, tab[1, t * per + i] * BLK, low)
        first = tab[1, t * per] // per

        def k_tile(kt, carry):
            top, total, acc = carry
            kbase = pl.multiple_of(kt * TILE, TILE)
            s = nt(qt, ks[pl.ds(kbase, TILE), :]) * SCALE2
            kpos = col + kbase
            s = jnp.where((kpos >= low) & (kpos <= row + base), s, NEG)
            new = jnp.maximum(top, jnp.max(s, axis=1, keepdims=True))
            p = jnp.exp2(s - new)
            fade = jnp.exp2(top - new)
            total = total * fade + jnp.sum(p, axis=1, keepdims=True)
            acc = acc * fade + nn(p.astype(bf16), vs[pl.ds(kbase, TILE), :])
            return new, total, acc

        top, total, acc = lax.fori_loop(
            first,
            t + 1,
            k_tile,
            (
                jnp.full((TILE, 1), NEG, f32),
                jnp.zeros((TILE, 1), f32),
                jnp.zeros((TILE, HS), f32),
            ),
        )
        att[pl.ds(base, TILE), :] = (acc / total).astype(bf16)
        lse = jnp.broadcast_to(top + jnp.log2(total), (TILE, HS))
        lse_c[pl.ds(base, TILE), :] = lse
        lse_r[:, pl.ds(base, TILE)] = lse.T[0:8, :]
        return 0

    lax.fori_loop(0, (TOK // TILE) * active, q_tile, 0)


def backward_kernel(tab, *refs):
    arrays = refs[:8]
    qs, ks, vs, att, lse_c, lse_r, out, dos, corr_r, acc = refs[8:]
    active = tab[3, 0]
    for a in range(8):

        def place(i, _, a=a):
            src = pl.ds(pl.multiple_of(i * BLK, BLK), BLK)
            dst = pl.ds(pl.multiple_of(tab[0, a * 8 + i] * BLK, BLK), BLK)
            dos[dst, :] = arrays[a][src, :]
            return 0

        lax.fori_loop(0, 8, place, 0, unroll=True)
    tail = pl.ds(TOK, PAD - TOK)
    dos[tail, :] = jnp.zeros((PAD - TOK, HS), bf16)
    corr_r[:, tail] = jnp.zeros((8, PAD - TOK), f32)
    ones = jnp.ones((8, HS), bf16)

    def corr_tile(t, _):
        rows = pl.ds(pl.multiple_of(t * TILE, TILE), TILE)
        prod = dos[rows, :].astype(f32) * att[rows, :].astype(f32)
        high = prod.astype(bf16)
        rest = (prod - high.astype(f32)).astype(bf16)
        corr_r[:, rows] = nt(ones, high) + nt(ones, rest)
        return 0

    lax.fori_loop(0, (TOK // TILE) * active, corr_tile, 0)

    span = WIN * BLK
    row = lax.broadcasted_iota(jnp.int32, (BLK, span), 0)
    col = lax.broadcasted_iota(jnp.int32, (BLK, span), 1)
    group = 2

    def own_group(g, _):
        spots = []
        trips = jnp.int32(0)
        for u in range(group):
            p = tab[0, g * group + u]
            low, high = tab[1, p], tab[2, p]
            even = (p // 2) * 2
            trips = jnp.maximum(trips, (p - low + WIN) // WIN)
            trips = jnp.maximum(trips, (high - even + WIN - 1) // WIN)
            spots.append((p, low, high, even))
        acc[...] = jnp.zeros_like(acc)
        fixed = []
        for u in range(group):
            rows = pl.ds(pl.multiple_of(spots[u][0] * BLK, BLK), BLK)
            d_own = dos[rows, :]
            corr = jnp.sum(
                d_own.astype(f32) * att[rows, :].astype(f32), axis=1, keepdims=True
            )
            fixed.append((rows, corr))

        def window(j, _):
            for u in range(group):
                p, low, high, even = spots[u]
                rows, corr = fixed[u]
                q_own, k_own, v_own, d_own = qs[rows, :], ks[rows, :], vs[rows, :], dos[rows, :]
                kst = jnp.minimum(low + j * WIN, NBLK)
                keys = pl.ds(pl.multiple_of(kst * BLK, BLK), span)
                kw, vw = ks[keys, :], vs[keys, :]
                s = nt(q_own, kw) * SCALE2
                ok = col + kst * BLK <= row + p * BLK
                prob = jnp.where(ok, jnp.exp2(s - lse_c[rows, 0:1]), 0.0)
                gs = (prob * (nt(d_own, vw) - corr) * SCALE).astype(bf16)
                acc[u, 0] += nn(gs, kw)
                qst = jnp.minimum(even + j * WIN, NBLK)
                qbase = pl.multiple_of(qst * BLK, 2 * BLK)
                ask = pl.ds(qbase, span)
                qw, dw = qs[ask, :], dos[ask, :]
                s = nt(k_own, qw) * SCALE2
                qpos = col + qbase
                ok = (qpos >= row + p * BLK) & (qpos < high * BLK)
                prob = jnp.where(ok, jnp.exp2(s - lse_r[0:1, ask]), 0.0)
                gs = (prob * (nt(v_own, dw) - corr_r[0:1, ask]) * SCALE).astype(bf16)
                acc[u, 1] += nn(gs, qw)
                acc[u, 2] += nn(prob.astype(bf16), dw)
            return 0

        lax.fori_loop(0, trips, window, 0)
        for u in range(group):
            rows = pl.ds(pl.multiple_of((g * group + u) * BLK, BLK), BLK)
            for i in range(3):
                out[rows, i * HS : (i + 1) * HS] = acc[u, i].astype(bf16)
        return 0

    lax.fori_loop(0, (8 // group) * active, own_group, 0)


def join_kernel(pos, *refs):
    parts, outs = refs[:4], refs[4:]
    y = pos[0]
    for d in range(YS):
        head = lax.rem(y + d, YS)

        @pl.when(head < HEADS_HERE)
        def _(d=d, head=head):
            cols = pl.ds(pl.multiple_of(head * HS, HS), HS)
            for i in range(3):
                outs[i][:, cols] = parts[d][:, i * HS : (i + 1) * HS]


def call(kernel, outs, n_in, name, scratch=(), flops=0, size=0):
    return pl.pallas_call(
        kernel,
        out_shape=[jax.ShapeDtypeStruct(s, t) for s, t in outs],
        in_specs=[SM] + [VM] * n_in,
        out_specs=[VM] * len(outs),
        scratch_shapes=list(scratch),
        name=name,
        cost_estimate=pl.CostEstimate(
            flops=flops, bytes_accessed=size, transcendentals=0
        ),
        compiler_params=pltpu.CompilerParams(vmem_limit_bytes=60000 * 1024),
    )


def tables(clusters, x, y, c):
    ids = jnp.arange(NBLK, dtype=jnp.int32)
    less = clusters[None, :] < clusters[:, None]
    same = clusters[None, :] == clusters[:, None]
    before = less | (same & (ids[None, :] < ids[:, None]))
    rank = jnp.sum(before.astype(jnp.int32), axis=1)
    low = jnp.sum(less.astype(jnp.int32), axis=1)
    high = low + jnp.sum(same.astype(jnp.int32), axis=1)
    at = (rank[None, :] == ids[:, None]).astype(jnp.int32)
    low_at = jnp.sum(at * low[None, :], axis=1)
    high_at = jnp.sum(at * high[None, :], axis=1)
    half, dy, dx, dc = ids % 2, (ids // 2) % 4, (ids // 8) % 4, ids // 32
    source = (((x - dx) % XS) * YS + (y - dy) % YS) * CS + (c + dc) % CS
    block = source * 2 + half
    pick = (block[:, None] == ids[None, :]).astype(jnp.int32)
    rank_slot = jnp.sum(pick * rank[None, :], axis=1)
    active = jnp.where(y < HEADS_HERE, 1, 0) * jnp.ones((NBLK,), jnp.int32)
    return jnp.stack([rank_slot, low_at, high_at, active]).astype(jnp.int32)


def spread(chunks):
    got = [chunks[0]] + [to_heads(chunks[d], d) for d in range(1, YS)]
    mine = jnp.concatenate(got, axis=0)
    row = [mine] + [along_x(mine, d) for d in range(1, XS)]
    return row + [swap_core(a) for a in row]


def shards(query_rows, key_rows, value_rows, output_grad, out_weight, clusters):
    s = lax.axis_index("seq").astype(jnp.int32)
    z = lax.axis_index("head").astype(jnp.int32)
    x, y, c = s // (YS * CS), (s // CS) % YS, s % CS
    pos = jnp.stack([y, z])
    tab = tables(clusters, x, y, c)

    g1 = along_z(output_grad, 1)
    g7 = along_z(output_grad, -1)
    g2 = along_z(output_grad, 2)
    g6 = along_z(output_grad, -2)
    g3 = along_z(g2, 1)
    g5 = along_z(g6, -1)
    g4 = along_z(g2, 2)
    packed = call(
        pack_kernel, [((ROWS, 3 * HS), bf16)] * YS, 3, "pack", size=800_000
    )(pos, query_rows, key_rows, value_rows)
    gathered = spread(packed)

    grads = call(
        project_kernel,
        [((ROWS, HS), bf16)] * YS,
        9,
        "project",
        scratch=[pltpu.VMEM((ROWS, HEADS_HERE * HS), bf16)],
        flops=2 * ROWS * 5120 * 384,
        size=5_500_000,
    )(pos, output_grad, g1, g2, g3, g4, g5, g6, g7, out_weight)
    grads_all = spread(grads)

    kept = call(
        forward_kernel,
        [((PAD, HS), bf16)] * 3
        + [((TOK, HS), bf16), ((TOK, HS), f32), ((8, PAD), f32)],
        8,
        "forward",
        flops=4_000_000_000,
        size=10_000_000,
    )(tab, *gathered)
    out = call(
        backward_kernel,
        [((8 * BLK, 3 * HS), bf16)],
        14,
        "backward",
        scratch=[
            pltpu.VMEM((PAD, HS), bf16),
            pltpu.VMEM((8, PAD), f32),
            pltpu.VMEM((2, 3, BLK, HS), f32),
        ],
        flops=2_000_000_000,
        size=10_000_000,
    )(tab, *grads_all, *kept)[0]
    parts = [out[d * ROWS : (d + 1) * ROWS] for d in range(YS)]
    back = [parts[0]] + [from_heads(parts[d], d) for d in range(1, YS)]
    return tuple(
        call(
            join_kernel,
            [((ROWS, HEADS_HERE * HS), bf16)] * 3,
            4,
            "join",
            size=800_000,
        )(pos, *back)
    )


def solution(mesh):
    return jax.shard_map(
        shards,
        mesh=mesh,
        in_specs=(
            P("seq", "head"),
            P("seq", "head"),
            P("seq", "head"),
            P("seq", "head"),
            P(None, "head"),
            P(),
        ),
        out_specs=(P("seq", "head"), P("seq", "head"), P("seq", "head")),
        check_vma=False,
    )
```

```python
import functools

import jax
import jax.numpy as jnp
from jax import lax
from jax.experimental import pallas as pl
from jax.experimental.pallas import tpu as pltpu
from jax.sharding import PartitionSpec as P

HS = 128
BLK = 64
XS, YS, CS = 4, 4, 2
NSEQ = XS * YS * CS
NZ = 8
HEADS_HERE = 3
ROWS = 128
NBLK = 64
TOK = NBLK * BLK
WIN = 8
PAD = TOK + WIN * BLK
GROUP = 4
SCALE = HS**-0.5
SCALE2 = SCALE * 1.4426950408889634
NEG = -1e30


f32, bf16 = jnp.float32, jnp.bfloat16
VM = pl.BlockSpec(memory_space=pltpu.VMEM)
SM = pl.BlockSpec(memory_space=pltpu.SMEM)


def seq_id(x, y, c):
    return ((x % XS) * YS + (y % YS)) * CS + (c % CS)


COORDS = [(x, y, c) for x in range(XS) for y in range(YS) for c in range(CS)]


def to_heads(a, d):
    pairs = [
        (seq_id(x, y, c), seq_id(x, y + d, c))
        for x, y, c in COORDS
        if (y + d) % YS < HEADS_HERE
    ]
    return lax.ppermute(a, "seq", pairs)


def from_heads(a, d):
    pairs = [
        (seq_id(x, y, c), seq_id(x, y - d, c)) for x, y, c in COORDS if y < HEADS_HERE
    ]
    return lax.ppermute(a, "seq", pairs)


def along_x(a, d):
    pairs = [
        (seq_id(x, y, c), seq_id(x + d, y, c)) for x, y, c in COORDS if y < HEADS_HERE
    ]
    return lax.ppermute(a, "seq", pairs)


def swap_core(a):
    pairs = [
        (seq_id(x, y, c), seq_id(x, y, c + 1)) for x, y, c in COORDS if y < HEADS_HERE
    ]
    return lax.ppermute(a, "seq", pairs)


def along_z(a, d):
    return lax.ppermute(a, "head", [(z, (z + d) % NZ) for z in range(NZ)])


def nt(a, b):
    return lax.dot_general(a, b, (((1,), (1,)), ((), ())), preferred_element_type=f32)


def nn(a, b):
    return lax.dot_general(a, b, (((1,), (0,)), ((), ())), preferred_element_type=f32)


def head_slice(y, d):
    head = jnp.minimum(lax.rem(y + d, YS), HEADS_HERE - 1)
    return pl.ds(pl.multiple_of(head * HS, HS), HS)


def pack_kernel(pos, q, k, v, *outs):
    y = pos[0]
    for d in range(YS):
        cols = head_slice(y, d)
        outs[d][:, 0:HS] = q[:, cols]
        outs[d][:, HS : 2 * HS] = k[:, cols]
        outs[d][:, 2 * HS :] = v[:, cols]


def project_kernel(pos, *refs):
    parts, w, outs, keep = refs[:8], refs[8], refs[9:13], refs[13]
    y, z = pos[0], pos[1]
    depth = parts[0].shape[1]
    total = None
    for d in range(NZ):
        start = pl.multiple_of(lax.rem(z - d + NZ, NZ) * depth, depth)
        term = nn(parts[d][...], w[pl.ds(start, depth), :])
        total = term if total is None else total + term
    keep[...] = total.astype(bf16)
    for d in range(YS):
        outs[d][...] = keep[:, head_slice(y, d)]


def each_block(tab, a, fn):
    for i in range(8):
        fn(i, tab[0, a * 8 + i])


def rows_of(p):
    return pl.ds(pl.multiple_of(p * BLK, BLK), BLK)


def forward_kernel(tab, *refs):
    arrays = refs[:8]
    ks, vs, att, lse_c, lse_r = refs[8:]
    for a in range(8):

        def place(i, p, a=a):
            src = pl.ds(i * BLK, BLK)
            ks[rows_of(p), :] = arrays[a][src, HS : 2 * HS]
            vs[rows_of(p), :] = arrays[a][src, 2 * HS :]

        each_block(tab, a, place)
    tail = pl.ds(TOK, PAD - TOK)
    for ref in (ks, vs):
        ref[tail, :] = jnp.zeros((PAD - TOK, HS), bf16)
    span = WIN * BLK
    row = lax.broadcasted_iota(jnp.int32, (BLK, span), 0)
    col = lax.broadcasted_iota(jnp.int32, (BLK, span), 1)
    gap = col - row

    def own_group(g, _):
        spots = []
        trips = jnp.int32(0)
        for u in range(GROUP):
            p = tab[0, g * GROUP + u]
            low = tab[1, p]
            trips = jnp.maximum(trips, (p - low + WIN) // WIN)
            spots.append((p, low))
        own = [arrays[0][rows_of(g * GROUP + u), 0:HS] for u in range(GROUP)]

        def window(j, carry):
            out = []
            for u in range(GROUP):
                p, low = spots[u]
                top, total, acc = carry[u]
                kst = jnp.minimum(low + j * WIN, NBLK)
                keys = pl.ds(pl.multiple_of(kst * BLK, BLK), span)
                s = nt(own[u], ks[keys, :]) * SCALE2
                s = jnp.where(gap <= (p - kst) * BLK, s, NEG)
                new = jnp.maximum(top, jnp.max(s, axis=1, keepdims=True))
                e = jnp.exp2(s - new)
                fade = jnp.exp2(top - new)
                total = total * fade + jnp.sum(e, axis=1, keepdims=True)
                acc = acc * fade + nn(e.astype(bf16), vs[keys, :])
                out.append((new, total, acc))
            return tuple(out)

        start = tuple(
            (
                jnp.full((BLK, 1), NEG, f32),
                jnp.zeros((BLK, 1), f32),
                jnp.zeros((BLK, HS), f32),
            )
            for _ in range(GROUP)
        )
        done = lax.fori_loop(0, trips, window, start)
        for u in range(GROUP):
            top, total, acc = done[u]
            at = rows_of(g * GROUP + u)
            att[at, :] = (acc / total).astype(bf16)
            lse_c[at, :] = jnp.broadcast_to(top + jnp.log2(total), (BLK, HS))
        return 0

    lax.fori_loop(0, (8 // GROUP) * tab[3, 0], own_group, 0)
    for i in range(4):
        cols = slice(i * HS, (i + 1) * HS)
        lse_r[:, cols] = lse_c[cols, :].T[0:8, :]


def split3(v):
    high = v.astype(bf16).astype(f32)
    mid = (v - high).astype(bf16).astype(f32)
    return high, mid, (v - high - mid).astype(bf16).astype(f32)


def payload_kernel(pos, *refs):
    parts, att, lse_r, out = refs[:4], refs[4], refs[5], refs[6]
    ones = jnp.ones((8, HS), bf16)
    lines = []
    for d in range(4):
        rows = slice(d * ROWS, (d + 1) * ROWS)
        grad = parts[d][...]
        out[rows, :] = grad
        prod = grad.astype(f32) * att[rows, :].astype(f32)
        high = prod.astype(bf16)
        rest = (prod - high.astype(f32)).astype(bf16)
        lines.append(lse_r[0:1, rows])
        lines.append((nt(ones, high) + nt(ones, rest))[0:1, :])
    stat = jnp.concatenate(lines, axis=0)
    out[4 * ROWS :, :] = jnp.concatenate(
        [*split3(stat), jnp.zeros((8, HS), f32)], axis=0
    ).astype(bf16)


def query_kernel(tab, mine, grad, att, lse_c, ks, vs, out):
    span = WIN * BLK
    row = lax.broadcasted_iota(jnp.int32, (BLK, span), 0)
    col = lax.broadcasted_iota(jnp.int32, (BLK, span), 1)
    gap = col - row

    def own_group(g, _):
        spots = []
        trips = jnp.int32(0)
        for u in range(GROUP):
            p = tab[0, g * GROUP + u]
            low = tab[1, p]
            trips = jnp.maximum(trips, (p - low + WIN) // WIN)
            at = rows_of(g * GROUP + u)
            g_own = grad[at, :]
            corr = jnp.sum(
                g_own.astype(f32) * att[at, :].astype(f32), axis=1, keepdims=True
            )
            spots.append((p, low, mine[at, 0:HS], g_own, corr, lse_c[at, 0:1]))

        def window(j, carry):
            out = []
            for u in range(GROUP):
                p, low, q_own, g_own, corr, lse = spots[u]
                kst = jnp.minimum(low + j * WIN, NBLK)
                keys = pl.ds(pl.multiple_of(kst * BLK, BLK), span)
                kw = ks[keys, :]
                s = nt(q_own, kw) * SCALE2
                prob = jnp.where(gap <= (p - kst) * BLK, jnp.exp2(s - lse), 0.0)
                gs = (prob * (nt(g_own, vs[keys, :]) - corr) * SCALE).astype(bf16)
                out.append(carry[u] + nn(gs, kw))
            return tuple(out)

        start = tuple(jnp.zeros((BLK, HS), f32) for _ in range(GROUP))
        done = lax.fori_loop(0, trips, window, start)
        for u in range(GROUP):
            out[rows_of(g * GROUP + u), :] = done[u].astype(bf16)
        return 0

    lax.fori_loop(0, (8 // GROUP) * tab[3, 0], own_group, 0)


def key_kernel(tab, *refs):
    arrays, grads = refs[:8], refs[8:16]
    ks, vs, dq = refs[16:19]
    outs = refs[19:23]
    qs, dos, stat, acc = refs[23:]
    lane = lax.broadcasted_iota(jnp.int32, (2, HS), 1) // BLK
    for a in range(8):
        packed = grads[a][4 * ROWS :, :].astype(f32)
        stats = packed[0:8, :] + packed[8:16, :] + packed[16:24, :]
        turned = pltpu.roll(stats, BLK, 1)

        def place(i, p, a=a, stats=stats, turned=turned):
            src = pl.ds(i * BLK, BLK)
            qs[rows_of(p), :] = arrays[a][src, 0:HS]
            dos[rows_of(p), :] = grads[a][src, :]
            r = 2 * (i // 2)
            side = p % 2
            line = jnp.where(side == i % 2, stats[r : r + 2, :], turned[r : r + 2, :])
            old = stat[p // 2, 0:2, :]
            stat[p // 2, 0:2, :] = jnp.where(lane == side, line, old)

        each_block(tab, a, place)
    tail = pl.ds(TOK, PAD - TOK)
    for ref in (qs, dos):
        ref[tail, :] = jnp.zeros((PAD - TOK, HS), bf16)
    stat[NBLK // 2 :, :, :] = jnp.zeros(((PAD - TOK) // HS, 8, HS), f32)
    span = WIN * BLK
    row = lax.broadcasted_iota(jnp.int32, (BLK, span), 0)
    col = lax.broadcasted_iota(jnp.int32, (BLK, span), 1)
    gap = col - row

    def own_group(g, _):
        spots = []
        trips = jnp.int32(0)
        for u in range(GROUP):
            p = tab[0, g * GROUP + u]
            high = tab[2, p]
            even = (p // 2) * 2
            trips = jnp.maximum(trips, (high - even + WIN - 1) // WIN)
            spots.append((p, high, even, ks[rows_of(p), :], vs[rows_of(p), :]))

        def window(j, carry):
            out = []
            for u in range(GROUP):
                p, high, even, k_own, v_own = spots[u]
                qst = jnp.minimum(even + j * WIN, NBLK)
                ask = pl.ds(pl.multiple_of(qst * BLK, 2 * BLK), span)
                qw, dw = qs[ask, :], dos[ask, :]
                tile = qst // 2
                lse = jnp.concatenate(
                    [stat[tile + t, 0:1, :] for t in range(WIN // 2)], axis=1
                )
                corr = jnp.concatenate(
                    [stat[tile + t, 1:2, :] for t in range(WIN // 2)], axis=1
                )
                s = nt(k_own, qw) * SCALE2
                ok = (gap >= (p - qst) * BLK) & (col < (high - qst) * BLK)
                prob = jnp.where(ok, jnp.exp2(s - lse), 0.0)
                gs = (prob * (nt(v_own, dw) - corr) * SCALE).astype(bf16)
                dk, dv = carry[u]
                out.append((dk + nn(gs, qw), dv + nn(prob.astype(bf16), dw)))
            return tuple(out)

        start = tuple(
            (jnp.zeros((BLK, HS), f32), jnp.zeros((BLK, HS), f32)) for _ in range(GROUP)
        )
        done = lax.fori_loop(0, trips, window, start)
        for u in range(GROUP):
            for i in range(2):
                acc[rows_of(g * GROUP + u), i * HS : (i + 1) * HS] = done[u][i].astype(bf16)
        return 0

    lax.fori_loop(0, (8 // GROUP) * tab[3, 0], own_group, 0)
    for d in range(4):
        rows = slice(d * ROWS, (d + 1) * ROWS)
        outs[d][:, 0:HS] = dq[rows, :]
        outs[d][:, HS:] = acc[rows, :]


def join_kernel(pos, *refs):
    parts, outs = refs[:4], refs[4:]
    y = pos[0]
    for d in range(YS):
        head = lax.rem(y + d, YS)

        @pl.when(head < HEADS_HERE)
        def _(d=d, head=head):
            cols = pl.ds(pl.multiple_of(head * HS, HS), HS)
            for i in range(3):
                outs[i][:, cols] = parts[d][:, i * HS : (i + 1) * HS]


def call(kernel, outs, n_in, name, scratch=(), flops=0, size=0):
    return pl.pallas_call(
        kernel,
        out_shape=[jax.ShapeDtypeStruct(s, t) for s, t in outs],
        in_specs=[SM] + [VM] * n_in,
        out_specs=[VM] * len(outs),
        scratch_shapes=list(scratch),
        name=name,
        cost_estimate=pl.CostEstimate(
            flops=flops, bytes_accessed=size, transcendentals=0
        ),
        compiler_params=pltpu.CompilerParams(vmem_limit_bytes=20000 * 1024),
    )


def tables(clusters, x, y, c):
    ids = jnp.arange(NBLK, dtype=jnp.int32)
    less = clusters[None, :] < clusters[:, None]
    same = clusters[None, :] == clusters[:, None]
    before = less | (same & (ids[None, :] < ids[:, None]))
    rank = jnp.sum(before.astype(jnp.int32), axis=1)
    low = jnp.sum(less.astype(jnp.int32), axis=1)
    high = low + jnp.sum(same.astype(jnp.int32), axis=1)
    at = (rank[None, :] == ids[:, None]).astype(jnp.int32)
    low_at = jnp.sum(at * low[None, :], axis=1)
    high_at = jnp.sum(at * high[None, :], axis=1)
    half, dy, dx, dc = ids % 2, (ids // 2) % 4, (ids // 8) % 4, ids // 32
    source = (((x - dx) % XS) * YS + (y - dy) % YS) * CS + (c + dc) % CS
    block = source * 2 + half
    pick = (block[:, None] == ids[None, :]).astype(jnp.int32)
    rank_slot = jnp.sum(pick * rank[None, :], axis=1)
    active = jnp.where(y < HEADS_HERE, 1, 0) * jnp.ones((NBLK,), jnp.int32)
    return jnp.stack([rank_slot, low_at, high_at, active]).astype(jnp.int32)


def to_row(chunks):
    return [chunks[0]] + [to_heads(chunks[d], d) for d in range(1, YS)]


def to_all(mine):
    row = [mine] + [along_x(mine, d) for d in range(1, XS)]
    return row + [swap_core(a) for a in row]


def shards(query_rows, key_rows, value_rows, output_grad, out_weight, clusters):
    s = lax.axis_index("seq").astype(jnp.int32)
    z = lax.axis_index("head").astype(jnp.int32)
    x, y, c = s // (YS * CS), (s // CS) % YS, s % CS
    pos = jnp.stack([y, z])
    tab = tables(clusters, x, y, c)

    g1 = along_z(output_grad, 1)
    g7 = along_z(output_grad, -1)
    g2 = along_z(output_grad, 2)
    g6 = along_z(output_grad, -2)
    g3 = along_z(g2, 1)
    g5 = along_z(g6, -1)
    g4 = along_z(g2, 2)
    packed = call(
        pack_kernel, [((ROWS, 3 * HS), bf16)] * YS, 3, "pack", size=800_000
    )(pos, query_rows, key_rows, value_rows)
    gathered = to_all(jnp.concatenate(to_row(packed), axis=0))

    grads = call(
        project_kernel,
        [((ROWS, HS), bf16)] * YS,
        9,
        "project",
        scratch=[pltpu.VMEM((ROWS, HEADS_HERE * HS), bf16)],
        flops=2 * ROWS * 5120 * 384,
        size=5_500_000,
    )(pos, output_grad, g1, g2, g3, g4, g5, g6, g7, out_weight)
    grads_row = to_row(grads)

    own = 8 * BLK
    ks, vs, att, lse_c, lse_r = call(
        forward_kernel,
        [((PAD, HS), bf16)] * 2 + [((own, HS), bf16), ((own, HS), f32), ((8, own), f32)],
        8,
        "forward",
        flops=2_000_000_000,
        size=6_000_000,
    )(tab, *gathered)
    payload = call(
        payload_kernel,
        [((own + 32, HS), bf16)],
        6,
        "payload",
        size=500_000,
    )(pos, *grads_row, att, lse_r)[0]
    dq = call(
        query_kernel,
        [((own, HS), bf16)],
        6,
        "query",
        flops=2_000_000_000,
        size=3_000_000,
    )(tab, gathered[0], payload, att, lse_c, ks, vs)[0]
    parts = call(
        key_kernel,
        [((ROWS, 3 * HS), bf16)] * YS,
        19,
        "key",
        scratch=[
            pltpu.VMEM((PAD, HS), bf16),
            pltpu.VMEM((PAD, HS), bf16),
            pltpu.VMEM((PAD // HS, 8, HS), f32),
            pltpu.VMEM((own, 2 * HS), bf16),
        ],
        flops=4_000_000_000,
        size=6_000_000,
    )(tab, *gathered, *to_all(payload), ks, vs, dq)
    back = [parts[0]] + [from_heads(parts[d], d) for d in range(1, YS)]
    return tuple(
        call(
            join_kernel,
            [((ROWS, HEADS_HERE * HS), bf16)] * 3,
            4,
            "join",
            size=800_000,
        )(pos, *back)
    )


def solution(mesh):
    return jax.shard_map(
        shards,
        mesh=mesh,
        in_specs=(
            P("seq", "head"),
            P("seq", "head"),
            P("seq", "head"),
            P("seq", "head"),
            P(None, "head"),
            P(),
        ),
        out_specs=(P("seq", "head"), P("seq", "head"), P("seq", "head")),
        check_vma=False,
    )
```

```python
import functools

import jax
import jax.numpy as jnp
from jax import lax
from jax.experimental import pallas as pl
from jax.experimental.pallas import tpu as pltpu
from jax.sharding import PartitionSpec as P


HS = 128
BLK = 64
XS, YS, CS = 4, 4, 2
NZ = 8
HEADS_HERE = 3
ROWS = 128
NBLK = 64
TOK = NBLK * BLK
WIN = 8
PAD = TOK + WIN * BLK
GROUP = 4
SCALE = HS**-0.5
SCALE2 = SCALE * 1.4426950408889634
NEG = -1e30


f32, bf16 = jnp.float32, jnp.bfloat16
VM = pl.BlockSpec(memory_space=pltpu.VMEM)
SM = pl.BlockSpec(memory_space=pltpu.SMEM)
HBM = pl.BlockSpec(memory_space=pltpu.HBM)


def seq_id(x, y, c):
    return ((x % XS) * YS + (y % YS)) * CS + (c % CS)


COORDS = [(x, y, c) for x in range(XS) for y in range(YS) for c in range(CS)]


def to_heads(a, d):
    pairs = [
        (seq_id(x, y, c), seq_id(x, y + d, c))
        for x, y, c in COORDS
        if (y + d) % YS < HEADS_HERE
    ]
    return lax.ppermute(a, "seq", pairs)


def from_heads(a, d):
    pairs = [
        (seq_id(x, y, c), seq_id(x, y - d, c)) for x, y, c in COORDS if y < HEADS_HERE
    ]
    return lax.ppermute(a, "seq", pairs)


def along_x(a, d):
    pairs = [
        (seq_id(x, y, c), seq_id(x + d, y, c)) for x, y, c in COORDS if y < HEADS_HERE
    ]
    return lax.ppermute(a, "seq", pairs)


def swap_core(a):
    pairs = [
        (seq_id(x, y, c), seq_id(x, y, c + 1)) for x, y, c in COORDS if y < HEADS_HERE
    ]
    return lax.ppermute(a, "seq", pairs)


def along_z(a, d):
    return lax.ppermute(a, "head", [(z, (z + d) % NZ) for z in range(NZ)])


def nt(a, b):
    return lax.dot_general(a, b, (((1,), (1,)), ((), ())), preferred_element_type=f32)


def nn(a, b):
    return lax.dot_general(a, b, (((1,), (0,)), ((), ())), preferred_element_type=f32)


def head_slice(y, d):
    head = jnp.minimum(lax.rem(y + d, YS), HEADS_HERE - 1)
    return pl.ds(pl.multiple_of(head * HS, HS), HS)


def pack_kernel(pos, q, k, v, *outs):
    y = pos[0]
    for d in range(YS):
        cols = head_slice(y, d)
        outs[d][:, 0:HS] = q[:, cols]
        outs[d][:, HS : 2 * HS] = k[:, cols]
        outs[d][:, 2 * HS :] = v[:, cols]


def project_kernel(ds, last, pos, *refs):
    n = len(ds)
    parts, w, rest = refs[:n], refs[n], refs[n + 1 :]
    chunks, sems = rest[-2:]
    y, z = pos[0], pos[1]
    depth = parts[0].shape[1]
    copies = []
    for i, d in enumerate(ds):
        start = pl.multiple_of(lax.rem(z - d + NZ, NZ) * depth, depth)
        copy = pltpu.make_async_copy(
            w.at[pl.ds(start, depth), :], chunks.at[i], sems.at[i]
        )
        copy.start()
        copies.append(copy)
    total = rest[0][...] if last else None
    for i in range(n):
        copies[i].wait()
        term = nn(parts[i][...], chunks[i])
        total = term if total is None else total + term
    if last:
        outs, keep = rest[1:5], rest[5]
        keep[...] = total.astype(bf16)
        for d in range(YS):
            outs[d][...] = keep[:, head_slice(y, d)]
    else:
        rest[0][...] = total


def each_block(tab, side, fn):
    for i in range(32):
        fn(i, tab[0, side * 32 + i])


def rows_of(p):
    return pl.ds(pl.multiple_of(p * BLK, BLK), BLK)


def forward_kernel(tab, *refs):
    arrays = refs[:2]
    ks, vs, att, lse_c, lse_r = refs[2:]
    for a in range(2):

        def place(i, p, a=a):
            src = pl.ds(i * BLK, BLK)
            ks[rows_of(p), :] = arrays[a][src, HS : 2 * HS]
            vs[rows_of(p), :] = arrays[a][src, 2 * HS :]

        each_block(tab, a, place)
    tail = pl.ds(TOK, PAD - TOK)
    for ref in (ks, vs):
        ref[tail, :] = jnp.zeros((PAD - TOK, HS), bf16)
    span = WIN * BLK
    row = lax.broadcasted_iota(jnp.int32, (BLK, span), 0)
    col = lax.broadcasted_iota(jnp.int32, (BLK, span), 1)
    gap = col - row

    def own_group(g, _):
        spots = []
        trips = jnp.int32(0)
        for u in range(GROUP):
            p = tab[0, g * GROUP + u]
            low = tab[1, p]
            trips = jnp.maximum(trips, (p - low + WIN) // WIN)
            spots.append((p, low))
        own = [arrays[0][rows_of(g * GROUP + u), 0:HS] for u in range(GROUP)]

        def window(j, carry):
            out = []
            for u in range(GROUP):
                p, low = spots[u]
                top, total, acc = carry[u]
                kst = jnp.minimum(low + j * WIN, NBLK)
                keys = pl.ds(pl.multiple_of(kst * BLK, BLK), span)
                s = nt(own[u], ks[keys, :]) * SCALE2
                s = jnp.where(gap <= (p - kst) * BLK, s, NEG)
                new = jnp.maximum(top, jnp.max(s, axis=1, keepdims=True))
                e = jnp.exp2(s - new)
                fade = jnp.exp2(top - new)
                total = total * fade + jnp.sum(e, axis=1, keepdims=True)
                acc = acc * fade + nn(e.astype(bf16), vs[keys, :])
                out.append((new, total, acc))
            return tuple(out)

        start = tuple(
            (
                jnp.full((BLK, 1), NEG, f32),
                jnp.zeros((BLK, 1), f32),
                jnp.zeros((BLK, HS), f32),
            )
            for _ in range(GROUP)
        )
        done = lax.fori_loop(0, trips, window, start)
        for u in range(GROUP):
            top, total, acc = done[u]
            at = rows_of(g * GROUP + u)
            att[at, :] = (acc / total).astype(bf16)
            lse_c[at, :] = jnp.broadcast_to(top + jnp.log2(total), (BLK, HS))
        return 0

    lax.fori_loop(0, (8 // GROUP) * tab[3, 0], own_group, 0)
    for i in range(4):
        cols = slice(i * HS, (i + 1) * HS)
        lse_r[:, cols] = lse_c[cols, :].T[0:8, :]


def split3(v):
    high = v.astype(bf16).astype(f32)
    mid = (v - high).astype(bf16).astype(f32)
    return high, mid, (v - high - mid).astype(bf16).astype(f32)


def payload_kernel(pos, *refs):
    parts, att, lse_r, out = refs[:4], refs[4], refs[5], refs[6]
    ones = jnp.ones((8, HS), bf16)
    lines = []
    for d in range(4):
        rows = slice(d * ROWS, (d + 1) * ROWS)
        grad = parts[d][...]
        out[rows, :] = grad
        prod = grad.astype(f32) * att[rows, :].astype(f32)
        high = prod.astype(bf16)
        rest = (prod - high.astype(f32)).astype(bf16)
        lines.append(lse_r[0:1, rows])
        lines.append((nt(ones, high) + nt(ones, rest))[0:1, :])
    stat = jnp.concatenate(lines, axis=0)
    out[4 * ROWS :, :] = jnp.concatenate(
        [*split3(stat), jnp.zeros((8, HS), f32)], axis=0
    ).astype(bf16)


def query_kernel(tab, mine, grad, att, lse_c, ks, vs, out):
    span = WIN * BLK
    row = lax.broadcasted_iota(jnp.int32, (BLK, span), 0)
    col = lax.broadcasted_iota(jnp.int32, (BLK, span), 1)
    gap = col - row

    def own_group(g, _):
        spots = []
        trips = jnp.int32(0)
        for u in range(GROUP):
            p = tab[0, g * GROUP + u]
            low = tab[1, p]
            trips = jnp.maximum(trips, (p - low + WIN) // WIN)
            at = rows_of(g * GROUP + u)
            g_own = grad[at, :]
            corr = jnp.sum(
                g_own.astype(f32) * att[at, :].astype(f32), axis=1, keepdims=True
            )
            spots.append((p, low, mine[at, 0:HS], g_own, corr, lse_c[at, 0:1]))

        def window(j, carry):
            out = []
            for u in range(GROUP):
                p, low, q_own, g_own, corr, lse = spots[u]
                kst = jnp.minimum(low + j * WIN, NBLK)
                keys = pl.ds(pl.multiple_of(kst * BLK, BLK), span)
                kw = ks[keys, :]
                s = nt(q_own, kw) * SCALE2
                prob = jnp.where(gap <= (p - kst) * BLK, jnp.exp2(s - lse), 0.0)
                gs = (prob * (nt(g_own, vs[keys, :]) - corr) * SCALE).astype(bf16)
                out.append(carry[u] + nn(gs, kw))
            return tuple(out)

        start = tuple(jnp.zeros((BLK, HS), f32) for _ in range(GROUP))
        done = lax.fori_loop(0, trips, window, start)
        for u in range(GROUP):
            out[rows_of(g * GROUP + u), :] = done[u].astype(bf16)
        return 0

    lax.fori_loop(0, (8 // GROUP) * tab[3, 0], own_group, 0)


def key_kernel(tab, *refs):
    arrays, grads = refs[:2], refs[2:4]
    ks, vs, dq = refs[4:7]
    outs = refs[7:11]
    qs, dos, stat, acc = refs[11:]
    lane = lax.broadcasted_iota(jnp.int32, (2, HS), 1) // BLK
    unit = 4 * ROWS + 32
    for a in range(2):
        both = []
        for e in range(XS):
            packed = grads[a][e * unit + 4 * ROWS : (e + 1) * unit, :].astype(f32)
            stats = packed[0:8, :] + packed[8:16, :] + packed[16:24, :]
            both.append((stats, pltpu.roll(stats, BLK, 1)))

        def place(i, p, a=a, both=both):
            stats, turned = both[i // 8]
            qs[rows_of(p), :] = arrays[a][pl.ds(i * BLK, BLK), 0:HS]
            dos[rows_of(p), :] = grads[a][pl.ds(i // 8 * unit + i % 8 * BLK, BLK), :]
            r = 2 * (i % 8 // 2)
            side = p % 2
            line = jnp.where(side == i % 2, stats[r : r + 2, :], turned[r : r + 2, :])
            old = stat[p // 2, 0:2, :]
            stat[p // 2, 0:2, :] = jnp.where(lane == side, line, old)

        each_block(tab, a, place)
    tail = pl.ds(TOK, PAD - TOK)
    for ref in (qs, dos):
        ref[tail, :] = jnp.zeros((PAD - TOK, HS), bf16)
    stat[NBLK // 2 :, :, :] = jnp.zeros(((PAD - TOK) // HS, 8, HS), f32)
    span = WIN * BLK
    row = lax.broadcasted_iota(jnp.int32, (BLK, span), 0)
    col = lax.broadcasted_iota(jnp.int32, (BLK, span), 1)
    gap = col - row

    def own_group(g, _):
        spots = []
        trips = jnp.int32(0)
        for u in range(GROUP):
            p = tab[0, g * GROUP + u]
            high = tab[2, p]
            even = (p // 2) * 2
            trips = jnp.maximum(trips, (high - even + WIN - 1) // WIN)
            spots.append((p, high, even, ks[rows_of(p), :], vs[rows_of(p), :]))

        def window(j, carry):
            out = []
            for u in range(GROUP):
                p, high, even, k_own, v_own = spots[u]
                qst = jnp.minimum(even + j * WIN, NBLK)
                ask = pl.ds(pl.multiple_of(qst * BLK, 2 * BLK), span)
                qw, dw = qs[ask, :], dos[ask, :]
                tile = qst // 2
                lse = jnp.concatenate(
                    [stat[tile + t, 0:1, :] for t in range(WIN // 2)], axis=1
                )
                corr = jnp.concatenate(
                    [stat[tile + t, 1:2, :] for t in range(WIN // 2)], axis=1
                )
                s = nt(k_own, qw) * SCALE2
                ok = (gap >= (p - qst) * BLK) & (col < (high - qst) * BLK)
                prob = jnp.where(ok, jnp.exp2(s - lse), 0.0)
                gs = (prob * (nt(v_own, dw) - corr) * SCALE).astype(bf16)
                dk, dv = carry[u]
                out.append((dk + nn(gs, qw), dv + nn(prob.astype(bf16), dw)))
            return tuple(out)

        start = tuple(
            (jnp.zeros((BLK, HS), f32), jnp.zeros((BLK, HS), f32)) for _ in range(GROUP)
        )
        done = lax.fori_loop(0, trips, window, start)
        for u in range(GROUP):
            for i in range(2):
                acc[rows_of(g * GROUP + u), i * HS : (i + 1) * HS] = done[u][i].astype(bf16)
        return 0

    lax.fori_loop(0, (8 // GROUP) * tab[3, 0], own_group, 0)
    for d in range(4):
        rows = slice(d * ROWS, (d + 1) * ROWS)
        outs[d][:, 0:HS] = dq[rows, :]
        outs[d][:, HS:] = acc[rows, :]


def join_kernel(pos, *refs):
    parts, outs = refs[:4], refs[4:]
    y = pos[0]
    for d in range(YS):
        head = lax.rem(y + d, YS)

        @pl.when(head < HEADS_HERE)
        def _(d=d, head=head):
            cols = pl.ds(pl.multiple_of(head * HS, HS), HS)
            for i in range(3):
                outs[i][:, cols] = parts[d][:, i * HS : (i + 1) * HS]


def call(kernel, outs, n_in, scratch=(), flops=0, size=0, streamed=()):
    def run(*args):
        return pl.pallas_call(
            kernel,
            out_shape=[jax.ShapeDtypeStruct(s, t) for s, t in outs],
            in_specs=[SM] + [HBM if i in streamed else VM for i in range(n_in)],
            out_specs=[VM] * len(outs),
            scratch_shapes=list(scratch),
            cost_estimate=pl.CostEstimate(
                flops=flops, bytes_accessed=size, transcendentals=0
            ),
            compiler_params=pltpu.CompilerParams(vmem_limit_bytes=20000 * 1024),
        )(*args)

    return run


def tables(clusters, x, y, c):
    ids = jnp.arange(NBLK, dtype=jnp.int32)
    less = clusters[None, :] < clusters[:, None]
    same = clusters[None, :] == clusters[:, None]
    before = less | (same & (ids[None, :] < ids[:, None]))
    rank = jnp.sum(before.astype(jnp.int32), axis=1)
    low = jnp.sum(less.astype(jnp.int32), axis=1)
    high = low + jnp.sum(same.astype(jnp.int32), axis=1)
    at = (rank[None, :] == ids[:, None]).astype(jnp.int32)
    low_at = jnp.sum(at * low[None, :], axis=1)
    high_at = jnp.sum(at * high[None, :], axis=1)
    half, dy, dx, dc = ids % 2, (ids // 2) % 4, (ids // 8) % 4, ids // 32
    source = (((x - dx) % XS) * YS + (y - dy) % YS) * CS + (c + dc) % CS
    block = source * 2 + half
    pick = (block[:, None] == ids[None, :]).astype(jnp.int32)
    rank_slot = jnp.sum(pick * rank[None, :], axis=1)
    active = jnp.where(y < HEADS_HERE, 1, 0) * jnp.ones((NBLK,), jnp.int32)
    return jnp.stack([rank_slot, low_at, high_at, active]).astype(jnp.int32)


def to_row(chunks):
    return [chunks[0]] + [to_heads(chunks[d], d) for d in range(1, YS)]


def to_all(mine):
    row = jnp.concatenate([mine] + [along_x(mine, d) for d in range(1, XS)], axis=0)
    return row, swap_core(row)


def body(query_rows, key_rows, value_rows, output_grad, out_weight, clusters):
    s = lax.axis_index("seq").astype(jnp.int32)
    z = lax.axis_index("head").astype(jnp.int32)
    x, y, c = s // (YS * CS), (s // CS) % YS, s % CS
    pos = jnp.stack([y, z])
    tab = tables(clusters, x, y, c)

    g2 = along_z(output_grad, 2)
    g6 = along_z(output_grad, -2)
    g1 = along_z(output_grad, 1)
    g7 = along_z(output_grad, -1)
    g3 = along_z(g2, 1)
    g5 = along_z(g6, -1)
    g4 = along_z(g2, 2)
    packed = call(
        pack_kernel, [((ROWS, 3 * HS), bf16)] * YS, 3, size=800_000
    )(pos, query_rows, key_rows, value_rows)
    gathered = to_all(jnp.concatenate(to_row(packed), axis=0))

    depth, wide = output_grad.shape[1], HEADS_HERE * HS
    early = call(
        functools.partial(project_kernel, (0, 1, 7, 2, 6), False),
        [((ROWS, wide), f32)],
        6,
        scratch=[pltpu.VMEM((5, depth, wide), bf16), pltpu.SemaphoreType.DMA((5,))],
        flops=2 * ROWS * 5 * depth * wide,
        size=3_500_000,
        streamed=(5,),
    )(pos, output_grad, g1, g7, g2, g6, out_weight)[0]
    grads = call(
        functools.partial(project_kernel, (3, 5, 4), True),
        [((ROWS, HS), bf16)] * YS,
        5,
        scratch=[
            pltpu.VMEM((ROWS, wide), bf16),
            pltpu.VMEM((3, depth, wide), bf16),
            pltpu.SemaphoreType.DMA((3,)),
        ],
        flops=2 * ROWS * 3 * depth * wide,
        size=2_000_000,
        streamed=(3,),
    )(pos, g3, g5, g4, out_weight, early)
    grads_row = to_row(grads)

    own = 8 * BLK
    ks, vs, att, lse_c, lse_r = call(
        forward_kernel,
        [((PAD, HS), bf16)] * 2 + [((own, HS), bf16), ((own, HS), f32), ((8, own), f32)],
        2,
        flops=2_000_000_000,
        size=6_000_000,
    )(tab, *gathered)
    payload = call(
        payload_kernel, [((own + 32, HS), bf16)], 6, size=500_000
    )(pos, *grads_row, att, lse_r)[0]
    dq = call(
        query_kernel, [((own, HS), bf16)], 6, flops=2_000_000_000, size=3_000_000
    )(tab, gathered[0], payload, att, lse_c, ks, vs)[0]
    parts = call(
        key_kernel,
        [((ROWS, 3 * HS), bf16)] * YS,
        7,
        scratch=[
            pltpu.VMEM((PAD, HS), bf16),
            pltpu.VMEM((PAD, HS), bf16),
            pltpu.VMEM((PAD // HS, 8, HS), f32),
            pltpu.VMEM((own, 2 * HS), bf16),
        ],
        flops=4_000_000_000,
        size=6_000_000,
    )(tab, *gathered, *to_all(payload), ks, vs, dq)
    back = [parts[0]] + [from_heads(parts[d], d) for d in range(1, YS)]
    return tuple(
        call(
            join_kernel, [((ROWS, HEADS_HERE * HS), bf16)] * 3, 4, size=800_000
        )(pos, *back)
    )


def solution(mesh):
    return jax.shard_map(
        body,
        mesh=mesh,
        in_specs=(
            P("seq", "head"),
            P("seq", "head"),
            P("seq", "head"),
            P("seq", "head"),
            P(None, "head"),
            P(),
        ),
        out_specs=(P("seq", "head"), P("seq", "head"), P("seq", "head")),
        check_vma=False,
    )
```
